32 devices in a mesh: video: 2 (over y), space: 4 (over z), tm: 4 (over x, core).
Axes of the slice: x: 2, y: 2, z: 4, core: 2. Of those that a mesh axis runs over, the one named last changes fastest.
Arguments:
- spatial_q: bfloat16 [16, 16, 16, 1152], P(('video', 'tm'), 'space'), parts along dimension 0, may hold values from -17 to 17
- spatial_k: bfloat16 [16, 16, 16, 1152], P(('video', 'tm'), 'space'), parts along dimension 0, may hold values from -17 to 17
- spatial_v: bfloat16 [16, 16, 16, 1152], P(('video', 'tm'), 'space'), parts along dimension 0, may hold values from -6 to 6
- temporal_q: bfloat16 [16, 16, 16, 1152], P(('video', 'tm'), 'space'), parts along dimension 0, may hold values from -17 to 17
- temporal_k: bfloat16 [16, 16, 16, 1152], P(('video', 'tm'), 'space'), parts along dimension 0, may hold values from -17 to 17
- temporal_v: bfloat16 [16, 16, 16, 1152], P(('video', 'tm'), 'space'), parts along dimension 0, may hold values from -6 to 6
- key_lists: int32 [16, 8], replicated, may hold values from -1 to 15, as said below
Outputs:
- spatial_out: bfloat16 [16, 16, 16, 1152], P(('video', 'tm'), 'space'), parts along dimension 0
- temporal_out: bfloat16 [16, 16, 16, 1152], P(('video', 'tm'), 'space'), parts along dimension 0
The draws below stay inside these ranges and needn't reach their ends.
There are 2 independent parts, one for each index of `video`. The reference program is written for one: setup_inputs(seed, part) draws one part's arguments, and reference() takes and returns one part's arrays. A program takes and returns all parts, laid end to end along the dimension named above; an argument that names none is the same for every part. Nothing has to cross between parts.
Inputs may be any that keep to these rules, and one draw needn't show every extreme that they name: key_lists[r] names distinct tile rows within 4 rows of r, r itself first; the named entries come first and the rest are -1.
All inputs are finite; a program needn't handle non-finite values.
Results may differ from the reference program's by a relative error of at most 0.0037.
Values may be sent and summed in bfloat16 or wider, within the bound.
A program may use at most 64 MiB of HBM per device.

```python
import jax
import jax.numpy as jnp
from jax import lax

HEADS = 16
HEAD_DIM = 72
D = 1152
COLS = 16
FRAMES = 8
ROWS = 16
RADIUS = 4
LIST = 8


def drawn_pair(key):
    shape = (FRAMES, ROWS, COLS, D)
    first, second = jax.random.split(key, 2)
    queries = 1.5 * jnp.clip(jax.random.normal(first, shape, jnp.float32), -4.0, 4.0)
    keyset = jnp.clip(jax.random.normal(second, shape, jnp.float32), -4.0, 4.0)
    return (queries, keyset)


def draw_spatial_q(key, part):
    return drawn_pair(jax.random.fold_in(key, 101))[0].astype(jnp.bfloat16)


def draw_spatial_k(key, part):
    return drawn_pair(jax.random.fold_in(key, 101))[1].astype(jnp.bfloat16)


def draw_temporal_q(key, part):
    return drawn_pair(jax.random.fold_in(key, 202))[0].astype(jnp.bfloat16)


def draw_temporal_k(key, part):
    return drawn_pair(jax.random.fold_in(key, 202))[1].astype(jnp.bfloat16)


def draw_key_lists(key, part):
    span = 2 * RADIUS + 1
    offsets = jnp.arange(span, dtype=jnp.int32) - RADIUS
    splits = jax.random.split(key, ROWS + 2)
    orders = jax.vmap(lambda single: jax.random.permutation(single, span))(splits[:ROWS])
    shifted = offsets[orders]
    row_ids = jnp.arange(ROWS, dtype=jnp.int32)[:, None] + shifted
    inside = (row_ids >= 0) & (row_ids < ROWS)
    ranking = jnp.where(shifted == 0, 0, jnp.where(inside, 1, 2)) * 4096 + jnp.arange(span, dtype=jnp.int32)[None, :]
    sorter = jnp.argsort(ranking, axis=1)
    chosen = jnp.take_along_axis(row_ids, sorter, axis=1)[:, :LIST]
    room = jnp.minimum(jnp.sum(inside.astype(jnp.int32), axis=1), LIST)
    counts = jax.random.randint(splits[ROWS], (ROWS,), 1, LIST + 1)
    star = RADIUS + jax.random.randint(splits[ROWS + 1], (), 0, ROWS - 2 * RADIUS)
    counts = jnp.where(jnp.arange(ROWS, dtype=jnp.int32) == star, LIST, counts)
    counts = jnp.minimum(counts, room)
    filled = jnp.arange(LIST, dtype=jnp.int32)[None, :] < counts[:, None]
    return jnp.where(filled, chosen, -1).astype(jnp.int32)


def block_levels(own_key, dims, cuts, low, top_value):
    level = 1.0
    for dim, parts in cuts:
        steps = jax.random.uniform(jax.random.fold_in(jax.random.fold_in(own_key, 6), dim), (parts,), jnp.float32, low / len(cuts), top_value / len(cuts))
        level = level * jnp.repeat(jnp.exp(steps), dims[dim] // parts).reshape((-1,) + (1,) * (len(dims) - 1 - dim))
    return level


def normal_values(stream_key, dims, scale, limit, pieces=(), kind=jnp.bfloat16):
    result = scale * jax.random.normal(stream_key, dims, jnp.float32)
    if pieces:
        result = result * block_levels(stream_key, dims, pieces, -0.22, 0.18)
    return jnp.clip(result, -limit, limit).astype(kind)


def setup_inputs(seed: int = 0, part: int = 0) -> dict:
    keys = jax.random.split(jax.random.key(seed), 8)
    part_keys = jax.random.split(jax.random.fold_in(keys[7], part), 8)
    spatial_q = draw_spatial_q(jax.random.fold_in(jax.random.fold_in(keys[7], part), 71), part)
    spatial_k = draw_spatial_k(jax.random.fold_in(jax.random.fold_in(keys[7], part), 71), part)
    spatial_v = normal_values(part_keys[2], (FRAMES, ROWS, COLS, D), 1.0, 6.0, ((0, 4), (1, 4)))
    temporal_q = draw_temporal_q(jax.random.fold_in(jax.random.fold_in(keys[7], part), 71), part)
    temporal_k = draw_temporal_k(jax.random.fold_in(jax.random.fold_in(keys[7], part), 71), part)
    temporal_v = normal_values(part_keys[5], (FRAMES, ROWS, COLS, D), 1.0, 6.0, ((0, 4), (1, 4)))
    key_lists = draw_key_lists(jax.random.fold_in(keys[7], 71), part)
    return {"spatial_q": spatial_q, "spatial_k": spatial_k, "spatial_v": spatial_v, "temporal_q": temporal_q, "temporal_k": temporal_k, "temporal_v": temporal_v, "key_lists": key_lists}


big_negative = -1.0e30


def spatial_item(item_index, spatial_q, spatial_k, spatial_v, key_lists):
    frame_index = item_index // ROWS
    row_index = item_index % ROWS
    queries = spatial_q[frame_index, row_index].astype(jnp.float32).reshape(COLS, HEADS, HEAD_DIM)
    entries = key_lists[row_index]
    listed = entries >= 0
    safe_rows = jnp.where(listed, entries, 0).astype(jnp.int32)
    keyset = spatial_k[frame_index][safe_rows].astype(jnp.float32).reshape(LIST * COLS, HEADS, HEAD_DIM)
    values = spatial_v[frame_index][safe_rows].astype(jnp.float32).reshape(LIST * COLS, HEADS, HEAD_DIM)
    scores = jnp.einsum("chd,khd->hck", queries, keyset) * HEAD_DIM ** -0.5
    allowed = jnp.repeat(listed, COLS)[None, None, :]
    highest = jnp.max(jnp.where(allowed, scores, big_negative), axis=-1, keepdims=True)
    weights = jnp.where(allowed, jnp.exp(scores - highest), 0.0)
    totals = jnp.sum(weights, axis=-1)
    rounded = lax.optimization_barrier(weights.astype(jnp.bfloat16)).astype(jnp.float32)
    blended = jnp.einsum("hck,khd->chd", rounded, values) / jnp.transpose(totals)[:, :, None]
    return blended.reshape(COLS, D).astype(jnp.bfloat16)


def reference(spatial_q, spatial_k, spatial_v, temporal_q, temporal_k, temporal_v, key_lists):
    def one_item(item_index):
        return spatial_item(item_index, spatial_q, spatial_k, spatial_v, key_lists)

    spatial_out = lax.map(one_item, jnp.arange(FRAMES * ROWS, dtype=jnp.int32))
    spatial_out = spatial_out.reshape(FRAMES, ROWS, COLS, D)

    queries = temporal_q.astype(jnp.float32).reshape(FRAMES, ROWS * COLS, HEADS, HEAD_DIM)
    keyset = temporal_k.astype(jnp.float32).reshape(FRAMES, ROWS * COLS, HEADS, HEAD_DIM)
    values = temporal_v.astype(jnp.float32).reshape(FRAMES, ROWS * COLS, HEADS, HEAD_DIM)
    scores = jnp.einsum("flhd,elhd->lhfe", queries, keyset) * HEAD_DIM ** -0.5
    highest = jnp.max(scores, axis=-1, keepdims=True)
    weights = jnp.exp(scores - highest)
    totals = jnp.sum(weights, axis=-1)
    rounded = lax.optimization_barrier(weights.astype(jnp.bfloat16)).astype(jnp.float32)
    blended = jnp.einsum("lhfe,elhd->flhd", rounded, values) / jnp.transpose(totals, (2, 0, 1))[:, :, :, None]
    temporal_out = blended.reshape(FRAMES, ROWS, COLS, D).astype(jnp.bfloat16)
    return (spatial_out, temporal_out)
```

```python
import functools
import math

import jax
import jax.numpy as jnp
from jax import lax
from jax.experimental import pallas as pl
from jax.experimental.pallas import tpu as pltpu
from jax.sharding import PartitionSpec as P

HEAD_DIM = 72
LANES = 128
BIG_NEGATIVE = -1e30
MESH = pl.DeviceIdType.MESH


def head_windows(channels):
    heads = channels // HEAD_DIM
    groups = []
    h = 0
    while h < heads:
        base = (h * HEAD_DIM) // LANES
        base = min(base, channels // LANES - 2)
        group = []
        while h < heads and (h + 1) * HEAD_DIM <= (base + 2) * LANES:
            group.append(h)
            h += 1
        groups.append((base, group))
    return groups


CUTS = (5, 7)


def chunk_tiles(tiles):
    edges = [0] + [c for c in CUTS if c < tiles] + [tiles]
    return list(zip(edges[:-1], edges[1:]))


def flipped(index, j):
    bit = 1
    while bit <= j:
        if j & bit:
            index = index + bit - 2 * bit * ((index // bit) % 2)
        bit *= 2
    return index


def attend(problems):
    factor = HEAD_DIM ** (-0.5) * math.log2(math.e)
    insides = []
    scored = []
    for (base, group), load_q, load_k, _, _, bias, queries in problems:
        lane = lax.broadcasted_iota(jnp.int32, (queries, 2 * LANES), 1)
        q = load_q(base)
        inside = []
        for h in group:
            low = h * HEAD_DIM - base * LANES
            inside.append((lane >= low) & (lane < low + HEAD_DIM))
        stack = jnp.concatenate(
            [jnp.where(m, q, jnp.zeros_like(q)) for m in inside], axis=0
        )
        scores = lax.dot_general(
            stack, load_k(base), (((1,), (1,)), ((), ())), preferred_element_type=jnp.float32
        )
        scored.append(scores.reshape(len(group), queries, -1) * factor + bias[...][None])
        insides.append(inside)
    weighed = []
    for scores in scored:
        highest = jnp.max(scores, axis=-1, keepdims=True)
        weights = jnp.exp2(scores - highest)
        totals = jnp.sum(weights, axis=-1, keepdims=True)
        rounded = weights.astype(jnp.bfloat16).reshape(-1, weights.shape[-1])
        weighed.append((rounded, 1.0 / totals))
    for ((base, group), _, _, load_v, store, _, queries), (rounded, inverse), inside in zip(
        problems, weighed, insides
    ):
        blended = jnp.dot(rounded, load_v(base), preferred_element_type=jnp.float32)
        blended = blended.reshape(len(group), queries, 2 * LANES) * inverse
        merged = jnp.zeros((queries, 2 * LANES), jnp.float32)
        for n, m in enumerate(inside):
            merged = jnp.where(m, blended[n], merged)
        store(merged)


def kernel(
    space_count, tm_count, reach,
    sq, sk, sv, tq, tk, tv, lists, sov, tov,
    sqv, kwin, vwin, tqv, tkb, tvb, sbias, tbias, entry,
    zsend, zrecv, xsend, xrecv, zready, xready, load_sem,
):
    frames, rows, cols, channels = sqv.shape
    s = lax.axis_index("space")
    t = lax.axis_index("tm")
    entries = lists.shape[0]
    extent = (2 * reach + 1) * rows
    groups = head_windows(channels)
    tiles = channels // LANES
    chunks = chunk_tiles(tiles)
    needed_last = [
        max(c for c in range(len(chunks)) if chunks[c][0] < base + 2) for base, _ in groups
    ]

    direct = [1] + list(range(2, tm_count, 2))
    z_moves = []
    for d in range(1, reach + 1):
        z_moves.append((d, reach - d, 2 * (d - 1)))
        z_moves.append((-d, reach + d, 2 * (d - 1) + 1))

    def lanes(c):
        low, high = chunks[c]
        return pl.ds(low * LANES, (high - low) * LANES)

    def reaches(by):
        return s + by < space_count if by > 0 else s + by >= 0

    def z_copy(which, c, move):
        by, place, index = move
        src = (sk, sv)[which]
        dst = (kwin, vwin)[which]
        return pltpu.make_async_remote_copy(
            src_ref=src.at[:, :, :, lanes(c)],
            dst_ref=dst.at[:, pl.ds(place * rows, rows), :, lanes(c)],
            send_sem=zsend.at[which, c, index],
            recv_sem=zrecv.at[which, c, index],
            device_id={"space": s + by},
            device_id_type=MESH,
        )

    def x_copy(which, c, j):
        dst = (tkb, tvb)[which]
        if j in direct:
            src = (tk, tv)[which].at[:, :, :, lanes(c)]
            peer = flipped(t, j)
        else:
            src = dst.at[pl.ds((j - 1) * frames, frames), :, :, lanes(c)]
            peer = flipped(t, 1)
        return pltpu.make_async_remote_copy(
            src_ref=src,
            dst_ref=dst.at[pl.ds(j * frames, frames), :, :, lanes(c)],
            send_sem=xsend.at[which, c, j],
            recv_sem=xrecv.at[which, c, j],
            device_id={"tm": peer},
            device_id_type=MESH,
        )

    loads = []
    middle = pl.ds(reach * rows, rows)
    for n, (src, dst) in enumerate(
        [
            (tq, tqv),
            (tk, tkb.at[pl.ds(0, frames)]),
            (tv, tvb.at[pl.ds(0, frames)]),
            (sq, sqv),
            (sk, kwin.at[:, middle]),
            (sv, vwin.at[:, middle]),
            (lists, entry),
        ]
    ):
        loads.append(pltpu.make_async_copy(src, dst, load_sem.at[n]))

    def above(j):
        return flipped(t, j) > t

    def tell(semaphore, peer):
        pl.semaphore_signal(semaphore, inc=1, device_id=peer, device_id_type=MESH)

    barrier = pltpu.get_barrier_semaphore()
    peers = 0
    for j in direct:
        peers = peers + jnp.where(above(j), 0, 1)

        @pl.when(above(j))
        def _():
            tell(barrier, {"tm": flipped(t, j)})
    for d in range(1, reach + 1):
        peers = peers + jnp.where(reaches(-d), 1, 0)

        @pl.when(reaches(d))
        def _():
            tell(barrier, {"space": s + d})
    for copy in loads:
        copy.start()

    @pl.when(peers > 0)
    def _():
        pl.semaphore_wait(barrier, peers)

    def send_x(j):
        for c in range(len(chunks)):
            for which in (0, 1):
                x_copy(which, c, j).start()

    def send_z(move):
        for c in range(len(chunks)):
            for which in (0, 1):
                z_copy(which, c, move).start()

    for d in range(1, reach + 1):
        @pl.when(reaches(-d))
        def _():
            tell(zready.at[d - 1], {"space": s - d})
    for j in direct:
        @pl.when(jnp.logical_not(above(j)))
        def _():
            tell(xready.at[j], {"tm": flipped(t, j)})
    outward = direct[1:] + direct[:1]
    for move in z_moves:
        if move[0] < 0:
            @pl.when(reaches(move[0]))
            def _():
                send_z(move)
    for j in outward:
        @pl.when(jnp.logical_not(above(j)))
        def _():
            send_x(j)
    for j in outward:
        @pl.when(above(j))
        def _():
            pl.semaphore_wait(xready.at[j], 1)
            send_x(j)
    for move in z_moves:
        if move[0] > 0:
            @pl.when(reaches(move[0]))
            def _():
                pl.semaphore_wait(zready.at[move[0] - 1], 1)
                send_z(move)

    for by, place, _ in z_moves:
        @pl.when(jnp.logical_not(reaches(-by)))
        def _():
            zeros = jnp.zeros((frames, rows, cols, channels), jnp.bfloat16)
            kwin[:, pl.ds(place * rows, rows)] = zeros
            vwin[:, pl.ds(place * rows, rows)] = zeros

    loads.pop().wait()
    column = lax.broadcasted_iota(jnp.int32, (cols, extent * cols), 1)
    for i in range(rows):
        member = jnp.zeros((cols, extent * cols), jnp.float32) + BIG_NEGATIVE
        for e in range(entries):
            row = entry[e, s * rows + i]
            low = (row - (s - reach) * rows) * cols
            low = jnp.where(row >= 0, low, -extent * cols)
            member = jnp.where((column >= low) & (column < low + cols), 0.0, member)
        sbias[pl.ds(i * cols, cols)] = member
    shape = tbias.shape
    tbias[...] = jnp.where(
        lax.broadcasted_iota(jnp.int32, shape, 0) % cols
        == lax.broadcasted_iota(jnp.int32, shape, 1) % cols,
        0.0,
        BIG_NEGATIVE,
    )
    for copy in loads:
        copy.wait()

    def pair(base):
        return slice(base * LANES, (base + 2) * LANES)

    pending = {}

    def keep(name, number, merged, put):
        base = groups[number][0]
        upcoming = groups[number + 1][0] if number + 1 < len(groups) else tiles
        for tile in (base, base + 1):
            part = merged[:, (tile - base) * LANES : (tile - base + 1) * LANES]
            if (name, tile) in pending:
                part = pending.pop((name, tile)) + part
            if tile < upcoming:
                put(slice(tile * LANES, (tile + 1) * LANES), part.astype(jnp.bfloat16))
            else:
                pending[name, tile] = part

    def spatial(number, f):
        def store(merged):
            def put(where, value):
                sov[f, :, :, where] = value.reshape(rows, cols, LANES)

            keep(("s", f), number, merged, put)

        return (
            groups[number],
            lambda b: sqv[f, :, :, pair(b)].reshape(rows * cols, 2 * LANES),
            lambda b: kwin[f, :, :, pair(b)].reshape(extent * cols, 2 * LANES),
            lambda b: vwin[f, :, :, pair(b)].reshape(extent * cols, 2 * LANES),
            store, sbias, rows * cols,
        )

    def temporal(number, r):
        def store(merged):
            def put(where, value):
                tov[:, r, :, where] = value.reshape(frames, cols, LANES)

            keep(("t", r), number, merged, put)

        keys = tm_count * frames * cols
        return (
            groups[number],
            lambda b: tqv[:, r, :, pair(b)].reshape(frames * cols, 2 * LANES),
            lambda b: tkb[:, r, :, pair(b)].reshape(keys, 2 * LANES),
            lambda b: tvb[:, r, :, pair(b)].reshape(keys, 2 * LANES),
            store, tbias, frames * cols,
        )

    ready = [[g for g in range(len(groups)) if needed_last[g] == c] for c in range(len(chunks))]
    for c in range(len(chunks) + 1):
        if c < len(chunks):
            for j in direct[1:]:
                for which in (0, 1):
                    x_copy(which, c, j).wait_recv()
                    x_copy(which, c, j + 1).start()
            for move in z_moves:
                @pl.when(reaches(-move[0]))
                def _():
                    for which in (0, 1):
                        z_copy(which, c, move).wait_recv()
        near = ready[c] if c < len(chunks) else []
        far = ready[c - 1] if c > 0 else []
        for at in range(0, max(len(near), len(far)), 2):
            problems = [spatial(g, f) for g in near[at : at + 2] for f in range(frames)]
            if c > 0 and at == 0:
                for j in [1] + [j + 1 for j in direct[1:]]:
                    for which in (0, 1):
                        x_copy(which, c - 1, j).wait_recv()
            problems += [temporal(g, r) for g in far[at : at + 2] for r in range(rows)]
            attend(problems)

    for c in range(len(chunks)):
        for which in (0, 1):
            for j in range(1, tm_count):
                x_copy(which, c, j).wait_send()
    for move in z_moves:
        @pl.when(reaches(move[0]))
        def _():
            for c in range(len(chunks)):
                for which in (0, 1):
                    z_copy(which, c, move).wait_send()


def written(first, second, first_out, second_out, sem):
    copies = [
        pltpu.make_async_copy(first, first_out, sem.at[0]),
        pltpu.make_async_copy(second, second_out, sem.at[1]),
    ]
    for copy in copies:
        copy.start()
    for copy in copies:
        copy.wait()


def on_device(space_count, tm_count, sq, sk, sv, tq, tk, tv, lists):
    frames, rows, cols, channels = sq.shape
    reach = min(5, (space_count - 1) // 2)
    extent = (2 * reach + 1) * rows
    block = (frames, rows, cols, channels)
    window = (frames, extent, cols, channels)
    gathered = (tm_count * frames, rows, cols, channels)
    pieces = len(chunk_tiles(channels // LANES))
    bf16 = jnp.bfloat16
    any_spec = pl.BlockSpec(memory_space=pl.ANY)
    dma = pltpu.SemaphoreType.DMA
    results = pl.pallas_call(
        functools.partial(kernel, space_count, tm_count, reach),
        out_shape=(pltpu.VMEM(block, bf16), pltpu.VMEM(block, bf16)),
        in_specs=[any_spec] * 7,
        out_specs=(pl.BlockSpec(memory_space=pltpu.VMEM),) * 2,
        scratch_shapes=[
            pltpu.VMEM(block, bf16),
            pltpu.VMEM(window, bf16),
            pltpu.VMEM(window, bf16),
            pltpu.VMEM(block, bf16),
            pltpu.VMEM(gathered, bf16),
            pltpu.VMEM(gathered, bf16),
            pltpu.VMEM((rows * cols, extent * cols), jnp.float32),
            pltpu.VMEM((frames * cols, tm_count * frames * cols), jnp.float32),
            pltpu.SMEM(lists.shape[::-1], jnp.int32),
            dma((2, pieces, 2 * reach)),
            dma((2, pieces, 2 * reach)),
            dma((2, pieces, tm_count)),
            dma((2, pieces, tm_count)),
            pltpu.SemaphoreType.REGULAR((max(reach, 1),)),
            pltpu.SemaphoreType.REGULAR((tm_count,)),
            dma((7,)),
        ],
        compiler_params=pltpu.CompilerParams(collective_id=0, has_side_effects=True),
        name="attention",
    )(sq, sk, sv, tq, tk, tv, lists.T)
    return pl.pallas_call(
        written,
        out_shape=(jax.ShapeDtypeStruct(block, bf16), jax.ShapeDtypeStruct(block, bf16)),
        in_specs=[any_spec] * 2,
        out_specs=(any_spec, any_spec),
        scratch_shapes=[dma((2,))],
        name="written",
    )(*[pltpu.with_memory_space_constraint(x, pltpu.VMEM) for x in results])


def solution(mesh):
    block = P(("video", "tm"), "space", None, None)
    return jax.shard_map(
        functools.partial(on_device, mesh.shape["space"], mesh.shape["tm"]),
        mesh=mesh,
        in_specs=(block,) * 6 + (P(),),
        out_specs=(block, block),
        check_vma=False,
    )
```

```python
import functools
import math

import jax
import jax.numpy as jnp
from jax import lax
from jax.experimental import pallas as pl
from jax.experimental.pallas import tpu as pltpu
from jax.sharding import PartitionSpec as P

HEAD_DIM = 72
LANES = 128
BIG_NEGATIVE = -1e30
MESH = pl.DeviceIdType.MESH


def head_windows(channels):
    heads = channels // HEAD_DIM
    groups = []
    h = 0
    while h < heads:
        base = (h * HEAD_DIM) // LANES
        base = min(base, channels // LANES - 2)
        group = []
        while h < heads and (h + 1) * HEAD_DIM <= (base + 2) * LANES:
            group.append(h)
            h += 1
        groups.append((base, group))
    return groups


CUTS = (5, 8)


def chunk_tiles(tiles):
    edges = [0] + [c for c in CUTS if c < tiles] + [tiles]
    return list(zip(edges[:-1], edges[1:]))


def kept_rows(rows, tm_count):
    return rows - 1 if rows > 1 and tm_count > 2 else rows


def flipped(index, j):
    bit = 1
    while bit <= j:
        if j & bit:
            index = index + bit - 2 * bit * ((index // bit) % 2)
        bit *= 2
    return index


def attend(problems, between=None):
    factor = HEAD_DIM ** (-0.5) * math.log2(math.e)
    insides = []
    scored = []
    for (base, group), load_q, load_k, _, _, bias, queries, _ in problems:
        lane = lax.broadcasted_iota(jnp.int32, (queries, 2 * LANES), 1)
        q = load_q(base)
        inside = []
        for h in group:
            low = h * HEAD_DIM - base * LANES
            inside.append((lane >= low) & (lane < low + HEAD_DIM))
        stack = jnp.concatenate(
            [jnp.where(m, q, jnp.zeros_like(q)) for m in inside], axis=0
        )
        scores = lax.dot_general(
            stack, load_k(base), (((1,), (1,)), ((), ())), preferred_element_type=jnp.float32
        )
        scored.append(scores.reshape(len(group), queries, -1) * factor + bias[...][None])
        insides.append(inside)
    weighed = []
    for scores, (_, _, _, _, _, _, _, note) in zip(scored, problems):
        highest = jnp.max(scores, axis=-1, keepdims=True)
        weights = jnp.exp2(scores - highest)
        totals = jnp.sum(weights, axis=-1, keepdims=True)
        rounded = weights.astype(jnp.bfloat16).reshape(-1, weights.shape[-1])
        weighed.append((rounded, 1.0 / totals))
        if note is not None:
            note(highest + jnp.log(totals) * math.log2(math.e))
    if between is not None:
        between()
    for ((base, group), _, _, load_v, store, _, queries, _), (rounded, inverse), inside in zip(
        problems, weighed, insides
    ):
        blended = jnp.dot(rounded, load_v(base), preferred_element_type=jnp.float32)
        blended = blended.reshape(len(group), queries, 2 * LANES) * inverse
        merged = jnp.zeros((queries, 2 * LANES), jnp.float32)
        for n, m in enumerate(inside):
            merged = jnp.where(m, blended[n], merged)
        store(merged)


def kernel(
    space_count, tm_count, reach,
    sq, sk, sv, tq, tk, tv, lists, sov, tov,
    sqv, kwin, vwin, tqv, tkb, tvb, sbias, tbias, entry,
    asked, answer, answered, own, spread,
    zsend, zrecv, xsend, xrecv, qsend, qrecv, osend, orecv, zready, xready, load_sem,
):
    frames, rows, cols, channels = sqv.shape
    s = lax.axis_index("space")
    t = lax.axis_index("tm")
    entries = lists.shape[0]
    extent = (2 * reach + 1) * rows
    heads = channels // HEAD_DIM
    groups = head_windows(channels)
    tiles = channels // LANES
    chunks = chunk_tiles(tiles)
    needed_last = [
        max(c for c in range(len(chunks)) if chunks[c][0] < base + 2) for base, _ in groups
    ]

    direct = [1] + list(range(2, tm_count, 2))
    kept = kept_rows(rows, tm_count)
    lent = direct[1:] if kept < rows else []
    z_moves = []
    for d in range(1, reach + 1):
        z_moves.append((d, reach - d, 2 * (d - 1)))
        z_moves.append((-d, reach + d, 2 * (d - 1) + 1))

    def lanes(c):
        low, high = chunks[c]
        return pl.ds(low * LANES, (high - low) * LANES)

    def reaches(by):
        return s + by < space_count if by > 0 else s + by >= 0

    def z_copy(which, c, move):
        by, place, index = move
        src = (sk, sv)[which]
        dst = (kwin, vwin)[which]
        return pltpu.make_async_remote_copy(
            src_ref=src.at[:, :, :, lanes(c)],
            dst_ref=dst.at[:, pl.ds(place * rows, rows), :, lanes(c)],
            send_sem=zsend.at[which, c, index],
            recv_sem=zrecv.at[which, c, index],
            device_id={"space": s + by},
            device_id_type=MESH,
        )

    def x_copy(which, c, j):
        dst = (tkb, tvb)[which]
        here = pl.ds(0, rows if j == 1 else kept)
        if j in direct:
            src = (tk, tv)[which].at[:, here, :, lanes(c)]
            peer = flipped(t, j)
        else:
            src = dst.at[pl.ds((j - 1) * frames, frames), here, :, lanes(c)]
            peer = flipped(t, 1)
        return pltpu.make_async_remote_copy(
            src_ref=src,
            dst_ref=dst.at[pl.ds(j * frames, frames), here, :, lanes(c)],
            send_sem=xsend.at[which, c, j],
            recv_sem=xrecv.at[which, c, j],
            device_id={"tm": peer},
            device_id_type=MESH,
        )

    def q_copy(n):
        return pltpu.make_async_remote_copy(
            src_ref=tq.at[:, pl.ds(kept, 1)],
            dst_ref=asked.at[n],
            send_sem=qsend.at[n],
            recv_sem=qrecv.at[n],
            device_id={"tm": flipped(t, lent[n])},
            device_id_type=MESH,
        )

    def o_copy(n):
        return pltpu.make_async_remote_copy(
            src_ref=answer.at[n],
            dst_ref=answered.at[n],
            send_sem=osend.at[n],
            recv_sem=orecv.at[n],
            device_id={"tm": flipped(t, lent[n])},
            device_id_type=MESH,
        )

    loads = []
    middle = pl.ds(reach * rows, rows)
    for n, (src, dst) in enumerate(
        [
            (tq, tqv),
            (tk, tkb.at[pl.ds(0, frames)]),
            (tv, tvb.at[pl.ds(0, frames)]),
            (sq, sqv),
            (sk, kwin.at[:, middle]),
            (sv, vwin.at[:, middle]),
            (lists, entry),
        ]
    ):
        loads.append(pltpu.make_async_copy(src, dst, load_sem.at[n]))

    def above(j):
        return flipped(t, j) > t

    def tell(semaphore, peer):
        pl.semaphore_signal(semaphore, inc=1, device_id=peer, device_id_type=MESH)

    barrier = pltpu.get_barrier_semaphore()
    peers = 0
    for j in direct:
        peers = peers + jnp.where(above(j), 0, 1)

        @pl.when(above(j))
        def _():
            tell(barrier, {"tm": flipped(t, j)})
    for d in range(1, reach + 1):
        peers = peers + jnp.where(reaches(-d), 1, 0)

        @pl.when(reaches(d))
        def _():
            tell(barrier, {"space": s + d})
    for copy in loads:
        copy.start()

    @pl.when(peers > 0)
    def _():
        pl.semaphore_wait(barrier, peers)

    def send_x(j):
        if j in lent:
            q_copy(lent.index(j)).start()
        for c in range(len(chunks)):
            for which in (0, 1):
                x_copy(which, c, j).start()

    def send_z(move):
        for c in range(len(chunks)):
            for which in (0, 1):
                z_copy(which, c, move).start()

    for d in range(1, reach + 1):
        @pl.when(reaches(-d))
        def _():
            tell(zready.at[d - 1], {"space": s - d})
    for j in direct:
        @pl.when(jnp.logical_not(above(j)))
        def _():
            tell(xready.at[j], {"tm": flipped(t, j)})
    outward = direct
    for move in z_moves:
        if move[0] < 0:
            @pl.when(reaches(move[0]))
            def _():
                send_z(move)
    for j in outward:
        @pl.when(jnp.logical_not(above(j)))
        def _():
            send_x(j)
    for j in outward:
        @pl.when(above(j))
        def _():
            pl.semaphore_wait(xready.at[j], 1)
            send_x(j)
    for move in z_moves:
        if move[0] > 0:
            @pl.when(reaches(move[0]))
            def _():
                pl.semaphore_wait(zready.at[move[0] - 1], 1)
                send_z(move)

    for by, place, _ in z_moves:
        @pl.when(jnp.logical_not(reaches(-by)))
        def _():
            zeros = jnp.zeros((frames, rows, cols, channels), jnp.bfloat16)
            kwin[:, pl.ds(place * rows, rows)] = zeros
            vwin[:, pl.ds(place * rows, rows)] = zeros

    loads.pop().wait()
    column = lax.broadcasted_iota(jnp.int32, (cols, extent * cols), 1)
    for i in range(rows):
        member = jnp.zeros((cols, extent * cols), jnp.float32) + BIG_NEGATIVE
        for e in range(entries):
            row = entry[e, s * rows + i]
            low = (row - (s - reach) * rows) * cols
            low = jnp.where(row >= 0, low, -extent * cols)
            member = jnp.where((column >= low) & (column < low + cols), 0.0, member)
        sbias[pl.ds(i * cols, cols)] = member
    shape = tbias.shape
    tbias[...] = jnp.where(
        lax.broadcasted_iota(jnp.int32, shape, 0) % cols
        == lax.broadcasted_iota(jnp.int32, shape, 1) % cols,
        0.0,
        BIG_NEGATIVE,
    )
    if lent:
        row = lax.broadcasted_iota(jnp.int32, spread.shape, 0)
        low = lax.broadcasted_iota(jnp.int32, spread.shape, 1) - (row % heads) * HEAD_DIM
        spread[...] = jnp.where(
            (low >= 0) & (low < HEAD_DIM) & (row < 3 * heads), 1.0, 0.0
        ).astype(jnp.bfloat16)
    for copy in loads:
        copy.wait()

    def pair(base):
        return slice(base * LANES, (base + 2) * LANES)

    pending = {}

    def keep(name, number, merged, put):
        base = groups[number][0]
        upcoming = groups[number + 1][0] if number + 1 < len(groups) else tiles
        for tile in (base, base + 1):
            part = merged[:, (tile - base) * LANES : (tile - base + 1) * LANES]
            if (name, tile) in pending:
                part = pending.pop((name, tile)) + part
            if tile < upcoming:
                put(slice(tile * LANES, (tile + 1) * LANES), part)
            else:
                pending[name, tile] = part

    def spatial(number, f):
        def store(merged):
            def put(where, value):
                sov[f, :, :, where] = value.astype(jnp.bfloat16).reshape(rows, cols, LANES)

            keep(("s", f), number, merged, put)

        return (
            groups[number],
            lambda b: sqv[f, :, :, pair(b)].reshape(rows * cols, 2 * LANES),
            lambda b: kwin[f, :, :, pair(b)].reshape(extent * cols, 2 * LANES),
            lambda b: vwin[f, :, :, pair(b)].reshape(extent * cols, 2 * LANES),
            store, sbias, rows * cols, None,
        )

    def temporal(number, r):
        def store(merged):
            def put(where, value):
                tov[:, r, :, where] = value.astype(jnp.bfloat16).reshape(frames, cols, LANES)

            keep(("t", r), number, merged, put)

        keys = tm_count * frames * cols
        return (
            groups[number],
            lambda b: tqv[:, r, :, pair(b)].reshape(frames * cols, 2 * LANES),
            lambda b: tkb[:, r, :, pair(b)].reshape(keys, 2 * LANES),
            lambda b: tvb[:, r, :, pair(b)].reshape(keys, 2 * LANES),
            store, tbias, frames * cols, None,
        )

    tokens = frames * cols
    lane = lax.broadcasted_iota(jnp.int32, (tokens, LANES), 1)
    sums = {}

    def part(number, n):
        def store(merged):
            def put(where, value):
                if n < 0:
                    own[:, where] = value
                else:
                    value = value.astype(jnp.bfloat16)
                    answer[n, :, :, :, where] = value.reshape(frames, 1, cols, LANES)

            keep(("p", n), number, merged, put)

        def note(logs):
            known = sums.get(n, jnp.zeros((tokens, LANES), jnp.float32))
            for at, h in enumerate(groups[number][1]):
                known = jnp.where((lane % heads) == h, logs[at], known)
            sums[n] = known

        def load_q(b):
            if n < 0:
                return tqv[:, kept, :, pair(b)].reshape(tokens, 2 * LANES)
            return asked[n, :, :, :, pair(b)].reshape(tokens, 2 * LANES)

        return (
            groups[number], load_q,
            lambda b: tkb[: 2 * frames, kept, :, pair(b)].reshape(2 * tokens, 2 * LANES),
            lambda b: tvb[: 2 * frames, kept, :, pair(b)].reshape(2 * tokens, 2 * LANES),
            store, tbias.at[:, : 2 * tokens], tokens, note,
        )

    def three(total):
        first = total.astype(jnp.bfloat16)
        rest = total - first.astype(jnp.float32)
        second = rest.astype(jnp.bfloat16)
        third = (rest - second.astype(jnp.float32)).astype(jnp.bfloat16)
        none = jnp.zeros_like(first)
        terms = jnp.where(lane < 2 * heads, second, jnp.where(lane < 3 * heads, third, none))
        return jnp.where(lane < heads, first, terms)

    def wait_direct(c):
        for j in direct[1:]:
            for which in (0, 1):
                x_copy(which, c, j).wait_recv()
                x_copy(which, c, j + 1).start()

    def wait_relayed(c):
        for j in direct[1:]:
            for which in (0, 1):
                x_copy(which, c, j + 1).wait_recv()

    def wait_z(c, which):
        for move in z_moves:
            @pl.when(reaches(-move[0]))
            def _():
                z_copy(which, c, move).wait_recv()

    ready = [[g for g in range(len(groups)) if needed_last[g] == c] for c in range(len(chunks))]

    def across(c):
        wait_z(c, 0)
        for at in range(0, len(ready[c]), 2):
            problems = [spatial(g, f) for g in ready[c][at : at + 2] for f in range(frames)]
            attend(problems, functools.partial(wait_z, c, 1) if at == 0 else None)

    def along(c):
        wait_relayed(c)
        for at in range(0, len(ready[c]), 2):
            attend([temporal(g, r) for g in ready[c][at : at + 2] for r in range(kept)])

    for c in range(len(chunks)):
        for which in (0, 1):
            x_copy(which, c, 1).wait_recv()
    if lent:
        for n in range(len(lent)):
            q_copy(n).wait_recv()
        for at in range(0, len(groups), 2):
            numbers = range(at, min(at + 2, len(groups)))
            attend([part(g, n) for g in numbers for n in range(-1, len(lent))])
        for n in range(len(lent)):
            terms = three(sums[n]).reshape(frames, 1, cols, LANES)
            answer[n, :, :, :, channels:] = terms
        own_terms = three(sums[-1])

    def return_parts():
        for n in range(len(lent)):
            o_copy(n).start()

    last = len(chunks) - 1
    for c in range(len(chunks)):
        wait_direct(c)
        if c == max(last - 1, 0):
            return_parts()
        if c < last - 1:
            across(c)
        if c == last and c > 0:
            across(c - 1)
        along(c)
    across(last)

    if lent:
        for n in range(len(lent)):
            o_copy(n).wait_recv()

        def spread_out(terms):
            return jnp.dot(terms, spread[...], preferred_element_type=jnp.float32)

        logs = [spread_out(own_terms)]
        parts = [own[...]]
        for n in range(len(lent)):
            logs.append(spread_out(answered[n, :, :, :, channels:].reshape(tokens, LANES)))
            value = answered[n, :, :, :, :channels].reshape(tokens, channels)
            parts.append(value.astype(jnp.float32))
        highest = functools.reduce(jnp.maximum, logs)
        weights = [jnp.exp2(log - highest) for log in logs]
        total = functools.reduce(jnp.add, weights)
        mixed = functools.reduce(jnp.add, [w * p for w, p in zip(weights, parts)]) / total
        tov[:, kept] = mixed.astype(jnp.bfloat16).reshape(frames, cols, channels)

    for n in range(len(lent)):
        q_copy(n).wait_send()
        o_copy(n).wait_send()
    for c in range(len(chunks)):
        for which in (0, 1):
            for j in range(1, tm_count):
                x_copy(which, c, j).wait_send()
    for move in z_moves:
        @pl.when(reaches(move[0]))
        def _():
            for c in range(len(chunks)):
                for which in (0, 1):
                    z_copy(which, c, move).wait_send()


def written(first, second, first_out, second_out, sem):
    copies = [
        pltpu.make_async_copy(first, first_out, sem.at[0]),
        pltpu.make_async_copy(second, second_out, sem.at[1]),
    ]
    for copy in copies:
        copy.start()
    for copy in copies:
        copy.wait()


def on_device(space_count, tm_count, sq, sk, sv, tq, tk, tv, lists):
    frames, rows, cols, channels = sq.shape
    reach = min(5, (space_count - 1) // 2)
    extent = (2 * reach + 1) * rows
    block = (frames, rows, cols, channels)
    window = (frames, extent, cols, channels)
    gathered = (tm_count * frames, rows, cols, channels)
    pieces = len(chunk_tiles(channels // LANES))
    peers = max(1, (tm_count - 1) // 2)
    bf16 = jnp.bfloat16
    any_spec = pl.BlockSpec(memory_space=pl.ANY)
    dma = pltpu.SemaphoreType.DMA
    results = pl.pallas_call(
        functools.partial(kernel, space_count, tm_count, reach),
        out_shape=(pltpu.VMEM(block, bf16), pltpu.VMEM(block, bf16)),
        in_specs=[any_spec] * 7,
        out_specs=(pl.BlockSpec(memory_space=pltpu.VMEM),) * 2,
        scratch_shapes=[
            pltpu.VMEM(block, bf16),
            pltpu.VMEM(window, bf16),
            pltpu.VMEM(window, bf16),
            pltpu.VMEM(block, bf16),
            pltpu.VMEM(gathered, bf16),
            pltpu.VMEM(gathered, bf16),
            pltpu.VMEM((rows * cols, extent * cols), jnp.float32),
            pltpu.VMEM((frames * cols, tm_count * frames * cols), jnp.float32),
            pltpu.SMEM(lists.shape[::-1], jnp.int32),
            pltpu.VMEM((peers, frames, 1, cols, channels), bf16),
            pltpu.VMEM((peers, frames, 1, cols, channels + LANES), bf16),
            pltpu.VMEM((peers, frames, 1, cols, channels + LANES), bf16),
            pltpu.VMEM((frames * cols, channels), jnp.float32),
            pltpu.VMEM((LANES, channels), bf16),
            dma((2, pieces, 2 * reach)),
            dma((2, pieces, 2 * reach)),
            dma((2, pieces, tm_count)),
            dma((2, pieces, tm_count)),
            dma((peers,)),
            dma((peers,)),
            dma((peers,)),
            dma((peers,)),
            pltpu.SemaphoreType.REGULAR((max(reach, 1),)),
            pltpu.SemaphoreType.REGULAR((tm_count,)),
            dma((7,)),
        ],
        compiler_params=pltpu.CompilerParams(collective_id=0, has_side_effects=True),
        name="attention",
    )(sq, sk, sv, tq, tk, tv, lists.T)
    return pl.pallas_call(
        written,
        out_shape=(jax.ShapeDtypeStruct(block, bf16), jax.ShapeDtypeStruct(block, bf16)),
        in_specs=[any_spec] * 2,
        out_specs=(any_spec, any_spec),
        scratch_shapes=[dma((2,))],
        name="written",
    )(*[pltpu.with_memory_space_constraint(x, pltpu.VMEM) for x in results])


def solution(mesh):
    block = P(("video", "tm"), "space", None, None)
    return jax.shard_map(
        functools.partial(on_device, mesh.shape["space"], mesh.shape["tm"]),
        mesh=mesh,
        in_specs=(block,) * 6 + (P(),),
        out_specs=(block, block),
        check_vma=False,
    )
```

```python
import functools
import math

import jax
import jax.numpy as jnp
from jax import lax
from jax.experimental import pallas as pl
from jax.experimental.pallas import tpu as pltpu
from jax.sharding import PartitionSpec as P

HEAD_DIM = 72
LANES = 128
BIG_NEGATIVE = -1e30
MESH = pl.DeviceIdType.MESH


def head_windows(channels):
    heads = channels // HEAD_DIM
    groups = []
    h = 0
    while h < heads:
        base = (h * HEAD_DIM) // LANES
        base = min(base, channels // LANES - 2)
        group = []
        while h < heads and (h + 1) * HEAD_DIM <= (base + 2) * LANES:
            group.append(h)
            h += 1
        groups.append((base, group))
    return groups


CUTS = (5, 7)


def chunk_tiles(tiles):
    edges = [0] + [c for c in CUTS if c < tiles] + [tiles]
    return list(zip(edges[:-1], edges[1:]))


def kept_rows(rows, tm_count):
    return rows - 1 if rows > 1 and tm_count > 2 else rows


def flipped(index, j):
    bit = 1
    while bit <= j:
        if j & bit:
            index = index + bit - 2 * bit * ((index // bit) % 2)
        bit *= 2
    return index


def attend(problems, between=None):
    factor = HEAD_DIM ** (-0.5) * math.log2(math.e)
    insides = []
    scored = []
    for (base, group), load_q, load_k, _, _, bias, queries, _ in problems:
        lane = lax.broadcasted_iota(jnp.int32, (queries, 2 * LANES), 1)
        q = load_q(base)
        inside = []
        for h in group:
            low = h * HEAD_DIM - base * LANES
            inside.append((lane >= low) & (lane < low + HEAD_DIM))
        stack = jnp.concatenate(
            [jnp.where(m, q, jnp.zeros_like(q)) for m in inside], axis=0
        )
        scores = lax.dot_general(
            stack, load_k(base), (((1,), (1,)), ((), ())), preferred_element_type=jnp.float32
        )
        scored.append(scores.reshape(len(group), queries, -1) * factor + bias[...][None])
        insides.append(inside)
    weighed = []
    for scores, (_, _, _, _, _, _, _, note) in zip(scored, problems):
        highest = jnp.max(scores, axis=-1, keepdims=True)
        weights = jnp.exp2(scores - highest)
        totals = jnp.sum(weights, axis=-1, keepdims=True)
        rounded = weights.astype(jnp.bfloat16).reshape(-1, weights.shape[-1])
        weighed.append((rounded, 1.0 / totals))
        if note is not None:
            note(highest + jnp.log(totals) * math.log2(math.e))
    if between is not None:
        between()
    for ((base, group), _, _, load_v, store, _, queries, _), (rounded, inverse), inside in zip(
        problems, weighed, insides
    ):
        blended = jnp.dot(rounded, load_v(base), preferred_element_type=jnp.float32)
        blended = blended.reshape(len(group), queries, 2 * LANES) * inverse
        merged = jnp.zeros((queries, 2 * LANES), jnp.float32)
        for n, m in enumerate(inside):
            merged = jnp.where(m, blended[n], merged)
        store(merged)


def kernel(
    space_count, tm_count, reach,
    sq, sk, sv, tq, tk, tv, lists, sov, tov,
    sqv, kwin, vwin, tqv, tkb, tvb, sbias, tbias, entry,
    asked, answer, answered, own, spread,
    zsend, zrecv, xsend, xrecv, qsend, qrecv, osend, orecv, zready, xready, load_sem,
):
    frames, rows, cols, channels = sqv.shape
    s = lax.axis_index("space")
    t = lax.axis_index("tm")
    entries = lists.shape[0]
    extent = (2 * reach + 1) * rows
    heads = channels // HEAD_DIM
    groups = head_windows(channels)
    tiles = channels // LANES
    chunks = chunk_tiles(tiles)
    needed_last = [
        max(c for c in range(len(chunks)) if chunks[c][0] < base + 2) for base, _ in groups
    ]

    direct = [1] + list(range(2, tm_count, 2))
    kept = kept_rows(rows, tm_count)
    lent = direct[1:] if kept < rows else []
    z_moves = []
    for d in range(1, reach + 1):
        z_moves.append((d, reach - d, 2 * (d - 1)))
        z_moves.append((-d, reach + d, 2 * (d - 1) + 1))

    def lanes(c):
        low, high = chunks[c]
        return pl.ds(low * LANES, (high - low) * LANES)

    def reaches(by):
        return s + by < space_count if by > 0 else s + by >= 0

    def z_copy(which, c, move):
        by, place, index = move
        src = (sk, sv)[which]
        dst = (kwin, vwin)[which]
        return pltpu.make_async_remote_copy(
            src_ref=src.at[:, :, :, lanes(c)],
            dst_ref=dst.at[:, pl.ds(place * rows, rows), :, lanes(c)],
            send_sem=zsend.at[which, c, index],
            recv_sem=zrecv.at[which, c, index],
            device_id={"space": s + by},
            device_id_type=MESH,
        )

    def x_copy(which, c, j):
        dst = (tkb, tvb)[which]
        here = pl.ds(0, rows if j == 1 else kept)
        if j in direct:
            src = (tk, tv)[which].at[:, here, :, lanes(c)]
            peer = flipped(t, j)
        else:
            src = dst.at[pl.ds((j - 1) * frames, frames), here, :, lanes(c)]
            peer = flipped(t, 1)
        return pltpu.make_async_remote_copy(
            src_ref=src,
            dst_ref=dst.at[pl.ds(j * frames, frames), here, :, lanes(c)],
            send_sem=xsend.at[which, c, j],
            recv_sem=xrecv.at[which, c, j],
            device_id={"tm": peer},
            device_id_type=MESH,
        )

    def q_copy(n):
        return pltpu.make_async_remote_copy(
            src_ref=tq.at[:, pl.ds(kept, 1)],
            dst_ref=asked.at[n],
            send_sem=qsend.at[n],
            recv_sem=qrecv.at[n],
            device_id={"tm": flipped(t, lent[n])},
            device_id_type=MESH,
        )

    def o_copy(n):
        return pltpu.make_async_remote_copy(
            src_ref=answer.at[n],
            dst_ref=answered.at[n],
            send_sem=osend.at[n],
            recv_sem=orecv.at[n],
            device_id={"tm": flipped(t, lent[n])},
            device_id_type=MESH,
        )

    loads = []
    middle = pl.ds(reach * rows, rows)
    for n, (src, dst) in enumerate(
        [
            (tq, tqv),
            (tk, tkb.at[pl.ds(0, frames)]),
            (tv, tvb.at[pl.ds(0, frames)]),
            (sq, sqv),
            (sk, kwin.at[:, middle]),
            (sv, vwin.at[:, middle]),
            (lists, entry),
        ]
    ):
        loads.append(pltpu.make_async_copy(src, dst, load_sem.at[n]))

    def above(j):
        return flipped(t, j) > t

    def tell(semaphore, peer):
        pl.semaphore_signal(semaphore, inc=1, device_id=peer, device_id_type=MESH)

    barrier = pltpu.get_barrier_semaphore()
    peers = 0
    for j in direct:
        peers = peers + jnp.where(above(j), 0, 1)

        @pl.when(above(j))
        def _():
            tell(barrier, {"tm": flipped(t, j)})
    for d in range(1, reach + 1):
        peers = peers + jnp.where(reaches(-d), 1, 0)

        @pl.when(reaches(d))
        def _():
            tell(barrier, {"space": s + d})
    for copy in loads:
        copy.start()

    @pl.when(peers > 0)
    def _():
        pl.semaphore_wait(barrier, peers)

    def send_x(j):
        if j in lent:
            q_copy(lent.index(j)).start()
        for c in range(len(chunks)):
            for which in (0, 1):
                x_copy(which, c, j).start()

    def send_z(move):
        for c in range(len(chunks)):
            for which in (0, 1):
                z_copy(which, c, move).start()

    for d in range(1, reach + 1):
        @pl.when(reaches(-d))
        def _():
            tell(zready.at[d - 1], {"space": s - d})
    for j in direct:
        @pl.when(jnp.logical_not(above(j)))
        def _():
            tell(xready.at[j], {"tm": flipped(t, j)})
    outward = direct
    for move in z_moves:
        if move[0] < 0:
            @pl.when(reaches(move[0]))
            def _():
                send_z(move)
    for j in outward:
        @pl.when(jnp.logical_not(above(j)))
        def _():
            send_x(j)
    for j in outward:
        @pl.when(above(j))
        def _():
            pl.semaphore_wait(xready.at[j], 1)
            send_x(j)
    for move in z_moves:
        if move[0] > 0:
            @pl.when(reaches(move[0]))
            def _():
                pl.semaphore_wait(zready.at[move[0] - 1], 1)
                send_z(move)

    for by, place, _ in z_moves:
        @pl.when(jnp.logical_not(reaches(-by)))
        def _():
            zeros = jnp.zeros((frames, rows, cols, channels), jnp.bfloat16)
            kwin[:, pl.ds(place * rows, rows)] = zeros
            vwin[:, pl.ds(place * rows, rows)] = zeros

    loads.pop().wait()
    column = lax.broadcasted_iota(jnp.int32, (cols, extent * cols), 1)
    for i in range(rows):
        member = jnp.zeros((cols, extent * cols), jnp.float32) + BIG_NEGATIVE
        for e in range(entries):
            row = entry[e, s * rows + i]
            low = (row - (s - reach) * rows) * cols
            low = jnp.where(row >= 0, low, -extent * cols)
            member = jnp.where((column >= low) & (column < low + cols), 0.0, member)
        sbias[pl.ds(i * cols, cols)] = member
    shape = tbias.shape
    tbias[...] = jnp.where(
        lax.broadcasted_iota(jnp.int32, shape, 0) % cols
        == lax.broadcasted_iota(jnp.int32, shape, 1) % cols,
        0.0,
        BIG_NEGATIVE,
    )
    if lent:
        row = lax.broadcasted_iota(jnp.int32, spread.shape, 0)
        low = lax.broadcasted_iota(jnp.int32, spread.shape, 1) - (row % heads) * HEAD_DIM
        spread[...] = jnp.where(
            (low >= 0) & (low < HEAD_DIM) & (row < 3 * heads), 1.0, 0.0
        ).astype(jnp.bfloat16)
    for copy in loads:
        copy.wait()

    def pair(base):
        return slice(base * LANES, (base + 2) * LANES)

    pending = {}

    def keep(name, number, merged, put):
        base = groups[number][0]
        upcoming = groups[number + 1][0] if number + 1 < len(groups) else tiles
        for tile in (base, base + 1):
            part = merged[:, (tile - base) * LANES : (tile - base + 1) * LANES]
            if (name, tile) in pending:
                part = pending.pop((name, tile)) + part
            if tile < upcoming:
                put(slice(tile * LANES, (tile + 1) * LANES), part)
            else:
                pending[name, tile] = part

    def spatial(number, f):
        def store(merged):
            def put(where, value):
                sov[f, :, :, where] = value.astype(jnp.bfloat16).reshape(rows, cols, LANES)

            keep(("s", f), number, merged, put)

        return (
            groups[number],
            lambda b: sqv[f, :, :, pair(b)].reshape(rows * cols, 2 * LANES),
            lambda b: kwin[f, :, :, pair(b)].reshape(extent * cols, 2 * LANES),
            lambda b: vwin[f, :, :, pair(b)].reshape(extent * cols, 2 * LANES),
            store, sbias, rows * cols, None,
        )

    def temporal(number, r):
        def store(merged):
            def put(where, value):
                tov[:, r, :, where] = value.astype(jnp.bfloat16).reshape(frames, cols, LANES)

            keep(("t", r), number, merged, put)

        keys = tm_count * frames * cols
        return (
            groups[number],
            lambda b: tqv[:, r, :, pair(b)].reshape(frames * cols, 2 * LANES),
            lambda b: tkb[:, r, :, pair(b)].reshape(keys, 2 * LANES),
            lambda b: tvb[:, r, :, pair(b)].reshape(keys, 2 * LANES),
            store, tbias, frames * cols, None,
        )

    tokens = frames * cols
    lane = lax.broadcasted_iota(jnp.int32, (tokens, LANES), 1)
    sums = {}

    def part(number, n):
        def store(merged):
            def put(where, value):
                if n < 0:
                    own[:, where] = value
                else:
                    value = value.astype(jnp.bfloat16)
                    answer[n, :, :, :, where] = value.reshape(frames, 1, cols, LANES)

            keep(("p", n), number, merged, put)

        def note(logs):
            known = sums.get(n, jnp.zeros((tokens, LANES), jnp.float32))
            for at, h in enumerate(groups[number][1]):
                known = jnp.where((lane % heads) == h, logs[at], known)
            sums[n] = known

        def load_q(b):
            if n < 0:
                return tqv[:, kept, :, pair(b)].reshape(tokens, 2 * LANES)
            return asked[n, :, :, :, pair(b)].reshape(tokens, 2 * LANES)

        return (
            groups[number], load_q,
            lambda b: tkb[: 2 * frames, kept, :, pair(b)].reshape(2 * tokens, 2 * LANES),
            lambda b: tvb[: 2 * frames, kept, :, pair(b)].reshape(2 * tokens, 2 * LANES),
            store, tbias.at[:, : 2 * tokens], tokens, note,
        )

    def three(total):
        first = total.astype(jnp.bfloat16)
        rest = total - first.astype(jnp.float32)
        second = rest.astype(jnp.bfloat16)
        third = (rest - second.astype(jnp.float32)).astype(jnp.bfloat16)
        none = jnp.zeros_like(first)
        terms = jnp.where(lane < 2 * heads, second, jnp.where(lane < 3 * heads, third, none))
        return jnp.where(lane < heads, first, terms)

    def spread_out(terms):
        return jnp.dot(terms, spread[...], preferred_element_type=jnp.float32)

    def wait_direct(c):
        for j in direct[1:]:
            for which in (0, 1):
                x_copy(which, c, j).wait_recv()
                x_copy(which, c, j + 1).start()

    def wait_relayed(c):
        for j in direct[1:]:
            for which in (0, 1):
                x_copy(which, c, j + 1).wait_recv()

    def wait_z(c, which):
        for move in z_moves:
            @pl.when(reaches(-move[0]))
            def _():
                z_copy(which, c, move).wait_recv()

    ready = [[g for g in range(len(groups)) if needed_last[g] == c] for c in range(len(chunks))]

    def across(c, beside=None):
        wait_z(c, 0)

        def arrive():
            if beside is not None:
                beside(c)
            wait_z(c, 1)

        for at in range(0, len(ready[c]), 2):
            problems = [spatial(g, f) for g in ready[c][at : at + 2] for f in range(frames)]
            attend(problems, arrive if at == 0 else None)

    def along(c):
        wait_relayed(c)
        for at in range(0, len(ready[c]), 2):
            attend([temporal(g, r) for g in ready[c][at : at + 2] for r in range(kept)])

    for c in range(len(chunks)):
        for which in (0, 1):
            x_copy(which, c, 1).wait_recv()
    if lent:
        for n in range(len(lent)):
            q_copy(n).wait_recv()
        for at in range(0, len(groups), 2):
            numbers = range(at, min(at + 2, len(groups)))
            attend([part(g, n) for g in numbers for n in range(-1, len(lent))])
        for n in range(len(lent)):
            terms = three(sums[n]).reshape(frames, 1, cols, LANES)
            answer[n, :, :, :, channels:] = terms
        own_logs = spread_out(three(sums[-1]))

    def return_parts():
        for n in range(len(lent)):
            o_copy(n).start()

    last = len(chunks) - 1
    for c in range(last):
        wait_direct(c)
        across(c)
        if c == 0:
            return_parts()
        along(c)
    wait_direct(last)
    if last == 0:
        return_parts()
    across(last, along)

    if lent:
        for n in range(len(lent)):
            o_copy(n).wait_recv()

        logs = [own_logs]
        parts = [own[...]]
        for n in range(len(lent)):
            logs.append(spread_out(answered[n, :, :, :, channels:].reshape(tokens, LANES)))
            value = answered[n, :, :, :, :channels].reshape(tokens, channels)
            parts.append(value.astype(jnp.float32))
        highest = functools.reduce(jnp.maximum, logs)
        weights = [jnp.exp2(log - highest) for log in logs]
        total = functools.reduce(jnp.add, weights)
        mixed = functools.reduce(jnp.add, [w * p for w, p in zip(weights, parts)]) / total
        tov[:, kept] = mixed.astype(jnp.bfloat16).reshape(frames, cols, channels)

    for n in range(len(lent)):
        q_copy(n).wait_send()
        o_copy(n).wait_send()
    for c in range(len(chunks)):
        for which in (0, 1):
            for j in range(1, tm_count):
                x_copy(which, c, j).wait_send()
    for move in z_moves:
        @pl.when(reaches(move[0]))
        def _():
            for c in range(len(chunks)):
                for which in (0, 1):
                    z_copy(which, c, move).wait_send()


def written(first, second, first_out, second_out, sem):
    copies = [
        pltpu.make_async_copy(first, first_out, sem.at[0]),
        pltpu.make_async_copy(second, second_out, sem.at[1]),
    ]
    for copy in copies:
        copy.start()
    for copy in copies:
        copy.wait()


def on_device(space_count, tm_count, sq, sk, sv, tq, tk, tv, lists):
    frames, rows, cols, channels = sq.shape
    reach = min(5, (space_count - 1) // 2)
    extent = (2 * reach + 1) * rows
    block = (frames, rows, cols, channels)
    window = (frames, extent, cols, channels)
    gathered = (tm_count * frames, rows, cols, channels)
    pieces = len(chunk_tiles(channels // LANES))
    peers = max(1, (tm_count - 1) // 2)
    bf16 = jnp.bfloat16
    any_spec = pl.BlockSpec(memory_space=pl.ANY)
    dma = pltpu.SemaphoreType.DMA
    results = pl.pallas_call(
        functools.partial(kernel, space_count, tm_count, reach),
        out_shape=(pltpu.VMEM(block, bf16), pltpu.VMEM(block, bf16)),
        in_specs=[any_spec] * 7,
        out_specs=(pl.BlockSpec(memory_space=pltpu.VMEM),) * 2,
        scratch_shapes=[
            pltpu.VMEM(block, bf16),
            pltpu.VMEM(window, bf16),
            pltpu.VMEM(window, bf16),
            pltpu.VMEM(block, bf16),
            pltpu.VMEM(gathered, bf16),
            pltpu.VMEM(gathered, bf16),
            pltpu.VMEM((rows * cols, extent * cols), jnp.float32),
            pltpu.VMEM((frames * cols, tm_count * frames * cols), jnp.float32),
            pltpu.SMEM(lists.shape[::-1], jnp.int32),
            pltpu.VMEM((peers, frames, 1, cols, channels), bf16),
            pltpu.VMEM((peers, frames, 1, cols, channels + LANES), bf16),
            pltpu.VMEM((peers, frames, 1, cols, channels + LANES), bf16),
            pltpu.VMEM((frames * cols, channels), jnp.float32),
            pltpu.VMEM((LANES, channels), bf16),
            dma((2, pieces, 2 * reach)),
            dma((2, pieces, 2 * reach)),
            dma((2, pieces, tm_count)),
            dma((2, pieces, tm_count)),
            dma((peers,)),
            dma((peers,)),
            dma((peers,)),
            dma((peers,)),
            pltpu.SemaphoreType.REGULAR((max(reach, 1),)),
            pltpu.SemaphoreType.REGULAR((tm_count,)),
            dma((7,)),
        ],
        compiler_params=pltpu.CompilerParams(collective_id=0, has_side_effects=True),
        name="attention",
    )(sq, sk, sv, tq, tk, tv, lists.T)
    return pl.pallas_call(
        written,
        out_shape=(jax.ShapeDtypeStruct(block, bf16), jax.ShapeDtypeStruct(block, bf16)),
        in_specs=[any_spec] * 2,
        out_specs=(any_spec, any_spec),
        scratch_shapes=[dma((2,))],
        name="written",
    )(*[pltpu.with_memory_space_constraint(x, pltpu.VMEM) for x in results])


def solution(mesh):
    block = P(("video", "tm"), "space", None, None)
    return jax.shard_map(
        functools.partial(on_device, mesh.shape["space"], mesh.shape["tm"]),
        mesh=mesh,
        in_specs=(block,) * 6 + (P(),),
        out_specs=(block, block),
        check_vma=False,
    )
```
